32 devices in a mesh: shot: 4 (over x, core), slab: 8 (over z, y).
Axes of the slice: x: 2, y: 2, z: 4, core: 2. Of those that a mesh axis runs over, the one named last changes fastest.
Arguments:
- fwd_prev: float32 [4, 256, 128, 128], P('shot', None, 'slab'), may hold values from -6 to 6
- fwd_now: float32 [4, 256, 128, 128], P('shot', None, 'slab'), may hold values from -6 to 6
- adj_late: float32 [4, 256, 128, 128], P('shot', None, 'slab'), may hold values from -6 to 6
- adj_last: float32 [4, 256, 128, 128], P('shot', None, 'slab'), may hold values from -6 to 6
- speed_model: float32 [512, 128, 128], P('shot', 'slab'), may hold values from 0.04 to 0.24
- anchors: int32 [4], replicated, may hold values from 0 to 256
- traces: float32 [8, 1024], P(None, ('shot', 'slab')), may hold values from -6 to 6
- dest: int32 [1024, 1], P(('shot', 'slab')), may hold values from 0 to 31; in each aligned block of 32 rows (0 to 31, 32 to 63, ...) at most 2 rows name the same one
- rec_pos: int32 [1024], P(('shot', 'slab')), may hold values from 0 to 4095
Outputs:
- image: float32 [512, 128, 128], P('shot', 'slab')
The draws below stay inside these ranges and needn't reach their ends.
Inputs may be any that keep to these rules, and one draw needn't show every extreme that they name: `dest`: within the rows of one device (aligned blocks of 32 receivers) no value occurs more than 2 times, and some value occurs exactly 2 times.
All inputs are finite; a program needn't handle non-finite values.
Results may differ from the reference program's by a relative error of at most 0.00002.
Values sent between devices are 32-bit elements; how exact they have to be, the bound alone decides.
A program may use at most 192 MiB of HBM per device.

```python
import math
import jax
import jax.numpy as jnp
import numpy as np
from jax import lax

CX = 16
AY = 256
NZ = 128
NSTEP = 8
CAP = 2
RDEPTH = 3
MX = 128
MY = 512
REC_DEV = 32
NREC = 1024
N_SHOT = 4
N_SLAB = 8
DEVICES = 32


def with_ends(drawn, stream_key, least, top_value):
    place = [jax.random.randint(jax.random.fold_in(stream_key, axis), (), 0, length) for axis, length in enumerate(drawn.shape)]
    widest = drawn.shape.index(max(drawn.shape))
    next_to = place[:widest] + [(place[widest] + 1) % drawn.shape[widest]] + place[widest + 1:]
    return drawn.at[tuple(place)].set(least).at[tuple(next_to)].set(top_value)


def block_scale(own_key, extent, shards, low, high):
    factor_of, own = 1.0, jax.random.fold_in(own_key, 6)
    for position, blocks in shards:
        steps = jnp.exp(jax.random.uniform(jax.random.fold_in(own, position), (blocks,), jnp.float32, low / len(shards), high / len(shards)))
        factor_of = factor_of * jnp.repeat(steps, extent[position] // blocks).reshape([-1 if axis == position else 1 for axis in range(len(extent))])
    return factor_of


def shared_out(stream_key, own, number, rows, number_of, top, reach, slope):
    sequence = jax.random.permutation(stream_key, number_of)
    heavy_load, usual = shares(number_of, rows * top, reach, slope, True), shares(number_of, rows * top, reach, slope, False)
    places = jnp.arange(number_of)

    def named(tallies, offset_by):
        used = int((tallies > 0).sum())
        fixed = max(1, used // 4)
        shifted = fixed + (places - fixed + offset_by * (used - fixed)) % max(1, number_of - fixed)
        return jnp.zeros((number_of,), jnp.int32).at[sequence[jnp.where(places < fixed, places, shifted)]].set(jnp.asarray(tallies, jnp.int32))

    tallies = jnp.where(number % 4 == 0, named(heavy_load, number // 4), named(usual, number - number // 4 - 1))
    mixed = jax.random.permutation(jax.random.fold_in(own, 3), number_of)
    source_of, receiver = mixed[0:number_of // 2 * 2:2], mixed[1:number_of // 2 * 2:2]
    slack = jnp.minimum(tallies[source_of] - 1, reach - tallies[receiver]) // 2
    slack = jnp.where((source_of == sequence[0]) | (receiver == sequence[0]) | (tallies[receiver] == 0), 0, jnp.maximum(slack, 0))
    shifted = jax.random.randint(jax.random.fold_in(own, 4), (number_of // 2,), 0, 1 << 20) % (slack + 1)
    tallies = tallies.at[source_of].add(-shifted).at[receiver].add(shifted)
    members = jnp.searchsorted(jnp.cumsum(tallies), jnp.arange(rows * top), side="right").astype(jnp.int32)
    table = members.reshape(top, rows).T
    table = table[jax.random.permutation(jax.random.fold_in(own, 1), rows)]
    offset_by = jax.random.randint(jax.random.fold_in(own, 2), (rows, 1), 0, top)
    return jnp.take_along_axis(table, (jnp.arange(top)[None, :] + offset_by) % top, axis=1)


def shares(count, total, limit, slope, full):
    portions = [(1 << 20) // math.isqrt(rank ** slope) + 1 for rank in range(1, count + 1)]
    largest = limit if full else min(limit, max(-(-total // count), total * portions[0] // sum(portions)))
    least = 1 if total - largest >= count - 1 else 0
    given, surplus = [largest] + [least] * (count - 1), total - largest - least * (count - 1)
    while surplus > 0:
        candidates = [i for i in range(1, count) if given[i] < largest] or [i for i in range(1, count) if given[i] < limit]
        mass, remaining = sum([portions[i] for i in candidates]), surplus
        for i in candidates:
            addition = min(limit - given[i], max(1, remaining * portions[i] // mass), surplus)
            given[i] = given[i] + addition
            surplus = surplus - addition
    return np.array(given)


def centred(rng, dims, spread, limit, pieces=(), dtype=jnp.bfloat16):
    loudness = block_scale(rng, dims, pieces, -0.22, 0.18) if pieces else 1.0
    array = jax.random.normal(rng, dims, jnp.float32) * spread * loudness
    return jnp.minimum(jnp.maximum(array, -limit), limit).astype(dtype)


def setup_inputs(seed: int = 0) -> dict:
    key_list = jax.random.split(jax.random.key(seed), 10)
    fwd_prev = centred(key_list[0], (N_SHOT, AY, MX, NZ), 1.0, 6.0, ((0, 4), (2, 8)), jnp.float32)
    fwd_now = centred(key_list[1], (N_SHOT, AY, MX, NZ), 1.0, 6.0, ((0, 4), (2, 8)), jnp.float32)
    adj_late = centred(key_list[2], (N_SHOT, AY, MX, NZ), 1.0, 6.0, ((0, 4), (2, 8)), jnp.float32)
    adj_last = centred(key_list[3], (N_SHOT, AY, MX, NZ), 1.0, 6.0, ((0, 4), (2, 8)), jnp.float32)
    speed_model = jnp.clip(jnp.exp(math.log(0.24) - 1.7917595 * jax.random.uniform(key_list[4], (MY, MX, NZ), jnp.float32) ** block_scale(key_list[4], (MY, MX, NZ), ((0, 4), (1, 8)), -0.2, 0.2)), 0.04, 0.24)
    anchors = with_ends(jax.random.randint(key_list[5], (N_SHOT,), 0, MY - AY + 1), jax.random.fold_in(key_list[5], 1), 0, MY - AY).astype(jnp.int32)
    traces = centred(key_list[6], (NSTEP, NREC), 1.0, 6.0, ((1, 32),), jnp.float32)
    dest_keys = jax.random.split(jax.random.fold_in(key_list[7], 1), NREC // REC_DEV)
    dest_turns = jax.random.permutation(jax.random.fold_in(key_list[7], 3), NREC // REC_DEV)
    dest = jax.vmap(lambda own, number: shared_out(jax.random.fold_in(key_list[7], 2), own, number, REC_DEV, DEVICES, 1, CAP, 2))(dest_keys, dest_turns).reshape((NREC, 1))
    rec_pos = with_ends(jax.random.randint(key_list[8], (NREC,), 0, AY * CX), jax.random.fold_in(key_list[8], 1), 0, (AY * CX) - 1).astype(jnp.int32)
    return {"fwd_prev": fwd_prev, "fwd_now": fwd_now, "adj_late": adj_late, "adj_last": adj_last, "speed_model": speed_model, "anchors": anchors, "traces": traces, "dest": dest, "rec_pos": rec_pos}


centre_coef = -2.5
near_coef = 4.0 / 3.0
far_coef = -1.0 / 12.0


def laplace(field):
    padded = jnp.pad(field, ((2, 2), (0, 0), (2, 2)))
    core = padded[2:-2, 2:-2, 2:-2]
    near = padded[1:-3, 2:-2, 2:-2] + padded[3:-1, 2:-2, 2:-2]
    near = near + padded[2:-2, 1:-3, 2:-2] + padded[2:-2, 3:-1, 2:-2]
    near = near + padded[2:-2, 2:-2, 1:-3] + padded[2:-2, 2:-2, 3:-1]
    far = padded[:-4, 2:-2, 2:-2] + padded[4:, 2:-2, 2:-2]
    far = far + padded[2:-2, :-4, 2:-2] + padded[2:-2, 4:, 2:-2]
    far = far + padded[2:-2, 2:-2, :-4] + padded[2:-2, 2:-2, 4:]
    return 3.0 * centre_coef * core + near_coef * near + far_coef * far


def full_laplace(field):
    return laplace(jnp.pad(field, ((0, 0), (2, 2), (0, 0))))


def reference(fwd_prev, fwd_now, adj_late, adj_last, speed_model, anchors, traces, dest, rec_pos):
    image = jnp.zeros((MY, MX, NZ), jnp.float32)
    target = dest[:, 0]
    for shot_index in range(N_SHOT):
        anchor = anchors[shot_index].astype(jnp.int32)
        speed = lax.dynamic_slice_in_dim(speed_model, anchor, AY, 0)
        prev, now = fwd_prev[shot_index], fwd_now[shot_index]
        snaps = []
        for step in range(NSTEP):
            nxt = 2.0 * now - prev + speed * full_laplace(now)
            prev, now = now, nxt
            snaps.append(now)
        chosen = (target // N_SLAB) == shot_index
        column = (target % N_SLAB) * CX + rec_pos % CX
        row = rec_pos // CX
        amounts = jnp.where(chosen[None, :], traces, jnp.float32(0.0))
        planes = jnp.zeros((NSTEP, AY, MX), jnp.float32).at[:, row, column].add(amounts)
        late, last = adj_late[shot_index], adj_last[shot_index]
        partial_value = jnp.zeros((AY, MX, NZ), jnp.float32)
        for level in range(NSTEP, 0, -1):
            drive = full_laplace(last).at[:, :, RDEPTH].add(planes[level - 1])
            current = 2.0 * last - late + speed * drive
            partial_value = partial_value + snaps[level - 1] * current
            late, last = last, current
        window = lax.dynamic_slice_in_dim(image, anchor, AY, 0)
        image = lax.dynamic_update_slice_in_dim(image, window + partial_value, anchor, 0)
    return image
```

```python
import functools

import jax
import jax.numpy as jnp
from jax import lax
from jax.experimental import pallas as pl
from jax.experimental.pallas import tpu as pltpu
from jax.sharding import PartitionSpec as P

NSTEP = 8
HALF = NSTEP // 2
CAP = 2
RDEPTH = 3
ROWS = 4
CHUNKS = 2
SLOTS = HALF + 2

centre_coef = -2.5
near_coef = 4.0 / 3.0
far_coef = -1.0 / 12.0

MESH = pl.DeviceIdType.MESH


def slot_of(n):
    late = (n + 1) // SLOTS
    return (n + 1) * (1 - late) + ((n + 1) % 2) * late


def wave_kernel(
    fwd_prev, fwd_now, adj_late, adj_last, speed_in, drive_in,
    out_ref,
    field, halo, edge, speed, drive,
    load_sem, send_sem, recv_sem,
):
    count = lax.axis_size("slab")
    me = lax.axis_index("slab")
    shot = lax.axis_index("shot")
    rows, cells, depth = speed.shape
    part = rows // CHUNKS

    loads = [
        pltpu.make_async_copy(fwd_now, field.at[0, 1, pl.ds(2, rows)], load_sem.at[0]),
        pltpu.make_async_copy(adj_last, field.at[1, 1, pl.ds(2, rows)], load_sem.at[1]),
        pltpu.make_async_copy(fwd_prev, field.at[0, 0, pl.ds(2, rows)], load_sem.at[2]),
        pltpu.make_async_copy(speed_in, speed, load_sem.at[3]),
        pltpu.make_async_copy(adj_late, field.at[1, 0, pl.ds(2, rows)], load_sem.at[4]),
        pltpu.make_async_copy(drive_in, drive, load_sem.at[5]),
    ]
    for load in loads:
        load.start()

    barrier = pltpu.get_barrier_semaphore()

    @pl.when(me > 0)
    def _():
        pl.semaphore_signal(barrier, inc=1, device_id=(shot, me - 1), device_id_type=MESH)

    @pl.when(me < count - 1)
    def _():
        pl.semaphore_signal(barrier, inc=1, device_id=(shot, me + 1), device_id_type=MESH)

    border = jnp.zeros((2, cells, depth), jnp.float32)
    for which in range(2):
        for slot in range(SLOTS):
            field[which, slot, 0:2] = border
            field[which, slot, rows + 2 : rows + 4] = border

    def clear(side):
        def body(i, carry):
            for which in range(2):
                for step in range(NSTEP):
                    halo[which, step, side, pl.ds(i * 16, 16)] = jnp.zeros(
                        (16, 2, depth), jnp.float32
                    )
            return carry

        lax.fori_loop(0, rows // 16, body, 0)

    @pl.when(me == 0)
    def _():
        clear(0)

    @pl.when(me == count - 1)
    def _():
        clear(1)

    peers = (me + count - 1) // count + (2 * count - 2 - me) // count
    pl.semaphore_wait(barrier, peers)

    def transfer(which, step, side, chunk):
        span = pl.ds(chunk * part, part)
        return pltpu.make_async_remote_copy(
            src_ref=edge.at[which, step, side, span],
            dst_ref=halo.at[which, step, 1 - side, span],
            send_sem=send_sem.at[which, step, side, chunk],
            recv_sem=recv_sem.at[which, step, 1 - side, chunk],
            device_id=(shot, me - 1 + 2 * side),
            device_id_type=MESH,
        )

    def send(which, step, chunk):
        @pl.when(me > 0)
        def _():
            transfer(which, step, 0, chunk).start()

        @pl.when(me < count - 1)
        def _():
            transfer(which, step, 1, chunk).start()

    def receive(which, step, chunk):
        @pl.when(me > 0)
        def _():
            transfer(which, step, 1, chunk).wait_recv()

        @pl.when(me < count - 1)
        def _():
            transfer(which, step, 0, chunk).wait_recv()

    for which in range(2):
        loads[which].wait()
        for chunk in range(CHUNKS):
            def pack(i, carry):
                y = chunk * part + i * 8
                cell = field[which, 1, pl.ds(y + 2, 8)]
                edge[which, 0, 0, pl.ds(y, 8)] = cell[:, 0:2]
                edge[which, 0, 1, pl.ds(y, 8)] = cell[:, cells - 2 : cells]
                return carry

            lax.fori_loop(0, part // 8, pack, 0)
            send(which, 0, chunk)

    for load in loads[2:]:
        load.wait()

    lane = lax.broadcasted_iota(jnp.int32, (ROWS, cells, depth), 2)

    def advance(which, k, image, last):
        newer, older, target = slot_of(k - 1), slot_of(k - 2), slot_of(k)
        partner = slot_of(k) if which == 0 else slot_of(NSTEP + 1 - k)
        for chunk in range(CHUNKS):
            receive(which, k - 1, chunk)

            def body(i, carry):
                y = chunk * part + i * ROWS
                window = field[which, newer, pl.ds(y, ROWS + 4)]
                core = window[2 : ROWS + 2]
                left = halo[which, k - 1, 0, pl.ds(y, ROWS)]
                right = halo[which, k - 1, 1, pl.ds(y, ROWS)]
                near = window[1 : ROWS + 1] + window[3 : ROWS + 3]
                far = window[0:ROWS] + window[4 : ROWS + 4]
                near = near + jnp.concatenate([left[:, 1:2], core[:, : cells - 1]], axis=1)
                near = near + jnp.concatenate([core[:, 1:], right[:, 0:1]], axis=1)
                far = far + jnp.concatenate([left, core[:, : cells - 2]], axis=1)
                far = far + jnp.concatenate([core[:, 2:], right], axis=1)
                near = near + jnp.where(lane >= 1, pltpu.roll(core, 1, 2), 0.0)
                near = near + jnp.where(lane < depth - 1, pltpu.roll(core, depth - 1, 2), 0.0)
                far = far + jnp.where(lane >= 2, pltpu.roll(core, 2, 2), 0.0)
                far = far + jnp.where(lane < depth - 2, pltpu.roll(core, depth - 2, 2), 0.0)
                lap = 3.0 * centre_coef * core + near_coef * near + far_coef * far
                if which == 1:
                    samples = drive[pl.ds(y, ROWS)]
                    shift = (RDEPTH - NSTEP + k + depth) % depth
                    lap = lap + jnp.where(lane == RDEPTH, pltpu.roll(samples, shift, 2), 0.0)
                older_cell = field[which, older, pl.ds(y + 2, ROWS)]
                value = 2.0 * core - older_cell + speed[pl.ds(y, ROWS)] * lap
                if image:
                    if which == 0:
                        other = field[1, slot_of(NSTEP + 1 - k), pl.ds(y + 2, ROWS)]
                    else:
                        other = field[0, slot_of(NSTEP + 1 - k), pl.ds(y + 2, ROWS)]
                    if image == "first" and which == 0:
                        out_ref[pl.ds(y, ROWS)] = value * other
                    else:
                        out_ref[pl.ds(y, ROWS)] = out_ref[pl.ds(y, ROWS)] + value * other
                if not last:
                    field[which, target, pl.ds(y + 2, ROWS)] = value
                    edge[which, k, 0, pl.ds(y, ROWS)] = value[:, 0:2]
                    edge[which, k, 1, pl.ds(y, ROWS)] = value[:, cells - 2 : cells]
                return carry

            lax.fori_loop(0, part // ROWS, body, 0)
            if not last:
                send(which, k, chunk)

    def early(k, carry):
        advance(0, k, None, False)
        advance(1, k, None, False)
        return carry

    lax.fori_loop(1, HALF + 1, early, 0)
    advance(0, HALF + 1, "first", False)
    advance(1, HALF + 1, "first", False)

    def later(k, carry):
        advance(0, k, "more", False)
        advance(1, k, "more", False)
        return carry

    lax.fori_loop(HALF + 2, NSTEP, later, 0)
    advance(0, NSTEP, "more", True)
    advance(1, NSTEP, "more", True)

    def settle(step, carry):
        for which in range(2):
            for chunk in range(CHUNKS):
                @pl.when(me > 0)
                def _():
                    transfer(which, step, 0, chunk).wait_send()

                @pl.when(me < count - 1)
                def _():
                    transfer(which, step, 1, chunk).wait_send()

        return carry

    lax.fori_loop(0, NSTEP, settle, 0)


def waves(prev, now, late, last, speed, drive):
    rows, cells, depth = now.shape
    anywhere = pl.BlockSpec(memory_space=pl.ANY)
    return pl.pallas_call(
        wave_kernel,
        out_shape=jax.ShapeDtypeStruct((rows, cells, depth), jnp.float32),
        in_specs=[anywhere] * 6,
        out_specs=pl.BlockSpec(memory_space=pltpu.VMEM),
        scratch_shapes=[
            pltpu.VMEM((2, SLOTS, rows + 4, cells, depth), jnp.float32),
            pltpu.VMEM((2, NSTEP, 2, rows, 2, depth), jnp.float32),
            pltpu.VMEM((2, NSTEP, 2, rows, 2, depth), jnp.float32),
            pltpu.VMEM((rows, cells, depth), jnp.float32),
            pltpu.VMEM((rows, cells, depth), jnp.float32),
            pltpu.SemaphoreType.DMA((6,)),
            pltpu.SemaphoreType.DMA((2, NSTEP, 2, CHUNKS)),
            pltpu.SemaphoreType.DMA((2, NSTEP, 2, CHUNKS)),
        ],
        compiler_params=pltpu.CompilerParams(
            collective_id=0, has_side_effects=True, vmem_limit_bytes=60 * 1024 * 1024
        ),
        name="waves",
    )(prev, now, late, last, speed, drive)


def per_device(fwd_prev, fwd_now, adj_late, adj_last, speed_model, anchors, traces, dest, rec_pos):
    prev, now = (fwd_prev[0], fwd_now[0])
    late, last = (adj_late[0], adj_last[0])
    aper_rows, slab_cols, depth = now.shape
    device_count = lax.axis_size("shot") * lax.axis_size("slab")
    anchor = lax.dynamic_index_in_dim(anchors, lax.axis_index("shot"), keepdims=False)
    piece = lax.all_gather(speed_model, "shot", axis=0, tiled=True)
    speed = lax.dynamic_slice_in_dim(piece, anchor, aper_rows, axis=0)

    target = dest[:, 0]
    onehot = (target[:, None] == jnp.arange(device_count, dtype=jnp.int32)[None, :]).astype(
        jnp.int32
    )
    rank = jnp.sum(onehot * (jnp.cumsum(onehot, axis=0) - 1), axis=1)
    slot = target * CAP + rank
    sample_buf = jnp.zeros((NSTEP, device_count * CAP), jnp.float32).at[:, slot].set(traces)
    place_buf = jnp.zeros((1, device_count * CAP), jnp.int32).at[0, slot].set(rec_pos)
    got_samples, got_places = (
        lax.all_to_all(sample_buf, ("shot", "slab"), split_axis=1, concat_axis=1, tiled=True),
        lax.all_to_all(place_buf, ("shot", "slab"), split_axis=1, concat_axis=1, tiled=True),
    )
    wide = jnp.pad(got_samples.T, ((0, 0), (0, depth - NSTEP)))
    drive = jnp.zeros((aper_rows * slab_cols, depth), jnp.float32).at[got_places[0]].add(wide)
    drive = drive.reshape(aper_rows, slab_cols, depth)

    partial_value = waves(prev, now, late, last, speed, drive)

    model_rows = speed_model.shape[0] * lax.axis_size("shot")
    placed = lax.dynamic_update_slice_in_dim(
        jnp.zeros((model_rows, slab_cols, depth), jnp.float32), partial_value, anchor, axis=0
    )
    return lax.psum_scatter(placed, "shot", scatter_dimension=0, tiled=True)


def solution(mesh):
    placed = (
        P("shot", None, "slab", None),
        P("shot", None, "slab", None),
        P("shot", None, "slab", None),
        P("shot", None, "slab", None),
        P("shot", "slab", None),
        P(),
        P(None, ("shot", "slab")),
        P(("shot", "slab"), None),
        P(("shot", "slab")),
    )
    return jax.shard_map(
        per_device, mesh=mesh, in_specs=placed, out_specs=P("shot", "slab", None), check_vma=False
    )
```

```python
import functools

import jax
import jax.numpy as jnp
from jax import lax
from jax.experimental import pallas as pl
from jax.experimental.pallas import tpu as pltpu
from jax.sharding import PartitionSpec as P

NSTEP = 8
HALF = NSTEP // 2
CAP = 2
RDEPTH = 3
ROWS = 4
CHUNKS = 2
SLOTS = HALF + 2
PIECES = 4
GROUP = 8

centre_coef = -2.5
near_coef = 4.0 / 3.0
far_coef = -1.0 / 12.0

MESH = pl.DeviceIdType.MESH


def slot_of(n):
    late = (n + 1) // SLOTS
    return (n + 1) * (1 - late) + ((n + 1) % 2) * late


def wave_kernel(
    anchors, fwd_prev, fwd_now, adj_late, adj_last, speed_in, drive_in,
    out_ref,
    field, halo, edge, model, drive, total, inbox, arrived,
    load_sem, send_sem, recv_sem, move_send, move_recv,
):
    count = lax.axis_size("slab")
    me = lax.axis_index("slab")
    shot = lax.axis_index("shot")
    rows, cells, depth = drive.shape
    block = out_ref.shape[0]
    piece = block // PIECES
    part = rows // CHUNKS
    core_index = shot % 2
    partner = shot + 1 - 2 * core_index
    across = (shot + 2) % 4
    beyond = (partner + 2) % 4
    anchor = anchors[shot]

    loads = [
        pltpu.make_async_copy(fwd_now, field.at[0, 1, pl.ds(2, rows)], load_sem.at[0]),
        pltpu.make_async_copy(adj_last, field.at[1, 1, pl.ds(2, rows)], load_sem.at[1]),
        pltpu.make_async_copy(fwd_prev, field.at[0, 0, pl.ds(2, rows)], load_sem.at[2]),
        pltpu.make_async_copy(speed_in, model.at[pl.ds(shot * block, block)], load_sem.at[3]),
        pltpu.make_async_copy(adj_late, field.at[1, 0, pl.ds(2, rows)], load_sem.at[4]),
        pltpu.make_async_copy(drive_in, drive, load_sem.at[5]),
    ]
    for load in loads:
        load.start()

    barrier = pltpu.get_barrier_semaphore()

    @pl.when(me > 0)
    def _():
        pl.semaphore_signal(barrier, inc=1, device_id=(shot, me - 1), device_id_type=MESH)

    @pl.when(me < count - 1)
    def _():
        pl.semaphore_signal(barrier, inc=1, device_id=(shot, me + 1), device_id_type=MESH)

    for other in (partner, across):
        pl.semaphore_signal(barrier, inc=1, device_id=(other, me), device_id_type=MESH)

    border = jnp.zeros((2, cells, depth), jnp.float32)
    total[0:GROUP] = jnp.zeros((GROUP, cells, depth), jnp.float32)
    total[rows + GROUP : rows + 2 * GROUP] = jnp.zeros((GROUP, cells, depth), jnp.float32)
    for which in range(2):
        for slot in range(SLOTS):
            field[which, slot, 0:2] = border
            field[which, slot, rows + 2 : rows + 4] = border

    def clear(side):
        def body(i, carry):
            for which in range(2):
                for step in range(NSTEP):
                    halo[which, step, side, pl.ds(i * 16, 16)] = jnp.zeros(
                        (16, 2, depth), jnp.float32
                    )
            return carry

        lax.fori_loop(0, rows // 16, body, 0)

    @pl.when(me == 0)
    def _():
        clear(0)

    @pl.when(me == count - 1)
    def _():
        clear(1)

    peers = (me + count - 1) // count + (2 * count - 2 - me) // count
    pl.semaphore_wait(barrier, peers + 2)

    def transfer(which, step, side, chunk):
        span = pl.ds(chunk * part, part)
        return pltpu.make_async_remote_copy(
            src_ref=edge.at[which, step, side, span],
            dst_ref=halo.at[which, step, 1 - side, span],
            send_sem=send_sem.at[which, step, side, chunk],
            recv_sem=recv_sem.at[which, step, 1 - side, chunk],
            device_id=(shot, me - 1 + 2 * side),
            device_id_type=MESH,
        )

    def send(which, step, chunk):
        @pl.when(me > 0)
        def _():
            transfer(which, step, 0, chunk).start()

        @pl.when(me < count - 1)
        def _():
            transfer(which, step, 1, chunk).start()

    def receive(which, step, chunk):
        @pl.when(me > 0)
        def _():
            transfer(which, step, 1, chunk).wait_recv()

        @pl.when(me < count - 1)
        def _():
            transfer(which, step, 0, chunk).wait_recv()

    def move(kind, p, source, target, device):
        return pltpu.make_async_remote_copy(
            src_ref=source,
            dst_ref=target,
            send_sem=move_send.at[kind, p],
            recv_sem=move_recv.at[kind, p],
            device_id=(device, me),
            device_id_type=MESH,
        )

    def model_across(p):
        span = model.at[pl.ds(shot * block + p * piece, piece)]
        return move(0, p, speed_in.at[pl.ds(p * piece, piece)], span, across)

    def model_partner(p):
        span = model.at[pl.ds(shot * block + p * piece, piece)]
        return move(1, p, speed_in.at[pl.ds(p * piece, piece)], span, partner)

    def model_onward(p):
        span = model.at[pl.ds(across * block + p * piece, piece)]
        return move(2, p, span, span, partner)

    for p in range(PIECES):
        model_across(p).start()

    for which in range(2):
        loads[which].wait()
        for chunk in range(CHUNKS):
            def pack(i, carry):
                y = chunk * part + i * 8
                cell = field[which, 1, pl.ds(y + 2, 8)]
                edge[which, 0, 0, pl.ds(y, 8)] = cell[:, 0:2]
                edge[which, 0, 1, pl.ds(y, 8)] = cell[:, cells - 2 : cells]
                return carry

            lax.fori_loop(0, part // 8, pack, 0)
            send(which, 0, chunk)

    for p in range(PIECES):
        model_partner(p).start()
    for load in loads[2:]:
        load.wait()
    for p in range(PIECES):
        model_across(p).wait_recv()
        model_onward(p).start()
    for p in range(PIECES):
        model_partner(p).wait_recv()
        model_onward(p).wait_recv()

    lane = lax.broadcasted_iota(jnp.int32, (ROWS, cells, depth), 2)

    def advance(which, k, image, last):
        newer, older, target = slot_of(k - 1), slot_of(k - 2), slot_of(k)
        partner = slot_of(k) if which == 0 else slot_of(NSTEP + 1 - k)
        for chunk in range(CHUNKS):
            receive(which, k - 1, chunk)

            def body(i, carry):
                y = chunk * part + i * ROWS
                window = field[which, newer, pl.ds(y, ROWS + 4)]
                core = window[2 : ROWS + 2]
                left = halo[which, k - 1, 0, pl.ds(y, ROWS)]
                right = halo[which, k - 1, 1, pl.ds(y, ROWS)]
                near = window[1 : ROWS + 1] + window[3 : ROWS + 3]
                far = window[0:ROWS] + window[4 : ROWS + 4]
                near = near + jnp.concatenate([left[:, 1:2], core[:, : cells - 1]], axis=1)
                near = near + jnp.concatenate([core[:, 1:], right[:, 0:1]], axis=1)
                far = far + jnp.concatenate([left, core[:, : cells - 2]], axis=1)
                far = far + jnp.concatenate([core[:, 2:], right], axis=1)
                near = near + jnp.where(lane >= 1, pltpu.roll(core, 1, 2), 0.0)
                near = near + jnp.where(lane < depth - 1, pltpu.roll(core, depth - 1, 2), 0.0)
                far = far + jnp.where(lane >= 2, pltpu.roll(core, 2, 2), 0.0)
                far = far + jnp.where(lane < depth - 2, pltpu.roll(core, depth - 2, 2), 0.0)
                lap = 3.0 * centre_coef * core + near_coef * near + far_coef * far
                if which == 1:
                    samples = drive[pl.ds(y, ROWS)]
                    shift = (RDEPTH - NSTEP + k + depth) % depth
                    lap = lap + jnp.where(lane == RDEPTH, pltpu.roll(samples, shift, 2), 0.0)
                older_cell = field[which, older, pl.ds(y + 2, ROWS)]
                value = 2.0 * core - older_cell + model[pl.ds(anchor + y, ROWS)] * lap
                if image:
                    if which == 0:
                        other = field[1, slot_of(NSTEP + 1 - k), pl.ds(y + 2, ROWS)]
                    else:
                        other = field[0, slot_of(NSTEP + 1 - k), pl.ds(y + 2, ROWS)]
                    if image == "first" and which == 0:
                        total[pl.ds(y + GROUP, ROWS)] = value * other
                    else:
                        total[pl.ds(y + GROUP, ROWS)] += value * other
                if not last:
                    field[which, target, pl.ds(y + 2, ROWS)] = value
                    edge[which, k, 0, pl.ds(y, ROWS)] = value[:, 0:2]
                    edge[which, k, 1, pl.ds(y, ROWS)] = value[:, cells - 2 : cells]
                return carry

            lax.fori_loop(0, part // ROWS, body, 0)
            if not last:
                send(which, k, chunk)

    def early(k, carry):
        advance(0, k, None, False)
        advance(1, k, None, False)
        return carry

    lax.fori_loop(1, HALF + 1, early, 0)
    advance(0, HALF + 1, "first", False)
    advance(1, HALF + 1, "first", False)

    def later(k, carry):
        advance(0, k, "more", False)
        advance(1, k, "more", False)
        return carry

    lax.fori_loop(HALF + 2, NSTEP, later, 0)
    advance(0, NSTEP, "more", True)
    advance(1, NSTEP, "more", True)

    for p in range(PIECES):
        model_across(p).wait_send()
        model_partner(p).wait_send()
        model_onward(p).wait_send()

    def share(owner, start):
        first = jnp.clip(owner * block + start - anchor, -GROUP, rows) + GROUP
        return total[pl.ds(first, GROUP)]

    def per_group(p, body):
        def run(i, carry):
            body(p * piece + i * GROUP)
            return carry

        lax.fori_loop(0, piece // GROUP, run, 0)

    def pair_copy(kind, p):
        return move(
            3 + kind, p,
            model.at[pl.ds(kind * block + p * piece, piece)],
            inbox.at[kind, pl.ds(p * piece, piece)],
            partner,
        )

    def far_copy(p):
        return move(
            5, p,
            model.at[pl.ds(2 * block + p * piece, piece)],
            arrived.at[pl.ds(p * piece, piece)],
            across,
        )

    for kind, owner in ((0, beyond), (1, partner)):
        for p in range(PIECES):
            def fill(y):
                model[pl.ds(kind * block + y, GROUP)] = share(owner, y)

            per_group(p, fill)
            pair_copy(kind, p).start()
        if kind == 0:
            for p in range(PIECES):
                pair_copy(0, p).wait_recv()

                def combine(y):
                    model[pl.ds(2 * block + y, GROUP)] = (
                        share(across, y) + inbox[0, pl.ds(y, GROUP)]
                    )

                per_group(p, combine)
                far_copy(p).start()
    for p in range(PIECES):
        pair_copy(1, p).wait_recv()

        def own(y):
            out_ref[pl.ds(y, GROUP)] = share(shot, y) + inbox[1, pl.ds(y, GROUP)]

        per_group(p, own)
    for p in range(PIECES):
        far_copy(p).wait_recv()

        def finish(y):
            out_ref[pl.ds(y, GROUP)] += arrived[pl.ds(y, GROUP)]

        per_group(p, finish)
    for p in range(PIECES):
        pair_copy(0, p).wait_send()
        pair_copy(1, p).wait_send()
        far_copy(p).wait_send()

    def settle(step, carry):
        for which in range(2):
            for chunk in range(CHUNKS):
                @pl.when(me > 0)
                def _():
                    transfer(which, step, 0, chunk).wait_send()

                @pl.when(me < count - 1)
                def _():
                    transfer(which, step, 1, chunk).wait_send()

        return carry

    lax.fori_loop(0, NSTEP, settle, 0)


def waves(anchors, prev, now, late, last, speed_model, drive):
    rows, cells, depth = now.shape
    block = speed_model.shape[0]
    model_rows = block * lax.axis_size("shot")
    anywhere = pl.BlockSpec(memory_space=pl.ANY)
    return pl.pallas_call(
        wave_kernel,
        out_shape=jax.ShapeDtypeStruct((block, cells, depth), jnp.float32),
        in_specs=[pl.BlockSpec(memory_space=pltpu.SMEM)] + [anywhere] * 6,
        out_specs=pl.BlockSpec(memory_space=pltpu.VMEM),
        scratch_shapes=[
            pltpu.VMEM((2, SLOTS, rows + 4, cells, depth), jnp.float32),
            pltpu.VMEM((2, NSTEP, 2, rows, 2, depth), jnp.float32),
            pltpu.VMEM((2, NSTEP, 2, rows, 2, depth), jnp.float32),
            pltpu.VMEM((model_rows, cells, depth), jnp.float32),
            pltpu.VMEM((rows, cells, depth), jnp.float32),
            pltpu.VMEM((rows + 2 * GROUP, cells, depth), jnp.float32),
            pltpu.VMEM((2, block, cells, depth), jnp.float32),
            pltpu.VMEM((block, cells, depth), jnp.float32),
            pltpu.SemaphoreType.DMA((6,)),
            pltpu.SemaphoreType.DMA((2, NSTEP, 2, CHUNKS)),
            pltpu.SemaphoreType.DMA((2, NSTEP, 2, CHUNKS)),
            pltpu.SemaphoreType.DMA((6, PIECES)),
            pltpu.SemaphoreType.DMA((6, PIECES)),
        ],
        compiler_params=pltpu.CompilerParams(
            collective_id=0, has_side_effects=True, vmem_limit_bytes=61 * 1024 * 1024
        ),
        name="waves",
    )(anchors, prev, now, late, last, speed_model, drive)


def per_device(fwd_prev, fwd_now, adj_late, adj_last, speed_model, anchors, traces, dest, rec_pos):
    prev, now = (fwd_prev[0], fwd_now[0])
    late, last = (adj_late[0], adj_last[0])
    aper_rows, slab_cols, depth = now.shape
    device_count = lax.axis_size("shot") * lax.axis_size("slab")

    target = dest[:, 0]
    listed = target.shape[0]
    index = jnp.arange(listed, dtype=jnp.int32)
    ahead = (target[:, None] == target[None, :]) & (index[None, :] < index[:, None])
    slot = target * CAP + jnp.sum(ahead.astype(jnp.int32), axis=1)
    listing = jnp.concatenate([traces, rec_pos.astype(jnp.float32)[None, :]], axis=0)
    sent = jnp.zeros((NSTEP + 1, device_count * CAP), jnp.float32).at[:, slot].set(listing)
    got = lax.all_to_all(sent, ("shot", "slab"), split_axis=1, concat_axis=1, tiled=True)
    places = got[NSTEP].astype(jnp.int32)
    wide = jnp.pad(got[:NSTEP].T, ((0, 0), (0, depth - NSTEP)))
    drive = jnp.zeros((aper_rows * slab_cols, depth), jnp.float32).at[places].add(wide)
    drive = drive.reshape(aper_rows, slab_cols, depth)
    return waves(anchors, prev, now, late, last, speed_model, drive)


def solution(mesh):
    placed = (
        P("shot", None, "slab", None),
        P("shot", None, "slab", None),
        P("shot", None, "slab", None),
        P("shot", None, "slab", None),
        P("shot", "slab", None),
        P(),
        P(None, ("shot", "slab")),
        P(("shot", "slab"), None),
        P(("shot", "slab")),
    )
    return jax.shard_map(
        per_device, mesh=mesh, in_specs=placed, out_specs=P("shot", "slab", None), check_vma=False
    )
```

```python
import functools

import jax
import jax.numpy as jnp
from jax import lax
from jax.experimental import pallas as pl
from jax.experimental.pallas import tpu as pltpu
from jax.sharding import PartitionSpec as P

NSTEP = 8
HALF = NSTEP // 2
CAP = 2
RDEPTH = 3
ROWS = 4
CHUNKS = 2
SLOTS = HALF + 2
PIECES = 4
GROUP = 8

centre_coef = -2.5
near_coef = 4.0 / 3.0
far_coef = -1.0 / 12.0

MESH = pl.DeviceIdType.MESH


def slot_of(n):
    late = (n + 1) // SLOTS
    return (n + 1) * (1 - late) + ((n + 1) % 2) * late


def wave_kernel(
    anchors, fwd_prev, fwd_now, adj_late, adj_last, speed_in, packet,
    out_ref,
    field, halo, edge, model, drive, total, inbox, arrived, gathered,
    load_sem, send_sem, recv_sem, move_send, move_recv,
    slab_send, slab_recv, shot_send, shot_recv,
):
    count = lax.axis_size("slab")
    me = lax.axis_index("slab")
    shot = lax.axis_index("shot")
    rows, cells, depth = drive.shape
    block = out_ref.shape[0]
    piece = block // PIECES
    part = rows // CHUNKS
    core_index = shot % 2
    partner = shot + 1 - 2 * core_index
    across = (shot + 2) % 4
    beyond = (partner + 2) % 4
    anchor = anchors[shot]

    loads = [
        pltpu.make_async_copy(fwd_now, field.at[0, 1, pl.ds(2, rows)], load_sem.at[0]),
        pltpu.make_async_copy(adj_last, field.at[1, 1, pl.ds(2, rows)], load_sem.at[1]),
        pltpu.make_async_copy(fwd_prev, field.at[0, 0, pl.ds(2, rows)], load_sem.at[2]),
        pltpu.make_async_copy(speed_in, model.at[pl.ds(shot * block, block)], load_sem.at[3]),
        pltpu.make_async_copy(adj_late, field.at[1, 0, pl.ds(2, rows)], load_sem.at[4]),
        pltpu.make_async_copy(packet.at[me], gathered.at[shot, me], load_sem.at[5]),
    ]
    for load in loads:
        load.start()

    barrier = pltpu.get_barrier_semaphore()

    shots = gathered.shape[0]

    def greet_slab(offset, carry):
        other = (me + offset) % count
        pl.semaphore_signal(barrier, inc=1, device_id=(shot, other), device_id_type=MESH)
        return carry

    def greet_shot(offset, carry):
        other = (shot + offset) % shots
        pl.semaphore_signal(barrier, inc=1, device_id=(other, me), device_id_type=MESH)
        return carry

    lax.fori_loop(1, count, greet_slab, 0)
    lax.fori_loop(1, shots, greet_shot, 0)

    border = jnp.zeros((2, cells, depth), jnp.float32)
    total[0:GROUP] = jnp.zeros((GROUP, cells, depth), jnp.float32)
    total[rows + GROUP : rows + 2 * GROUP] = jnp.zeros((GROUP, cells, depth), jnp.float32)
    for which in range(2):
        for slot in range(SLOTS):
            field[which, slot, 0:2] = border
            field[which, slot, rows + 2 : rows + 4] = border

    def clear(side):
        def body(i, carry):
            for which in range(2):
                for step in range(NSTEP):
                    halo[which, step, side, pl.ds(i * 16, 16)] = jnp.zeros(
                        (16, 2, depth), jnp.float32
                    )
            return carry

        lax.fori_loop(0, rows // 16, body, 0)

    @pl.when(me == 0)
    def _():
        clear(0)

    @pl.when(me == count - 1)
    def _():
        clear(1)

    pl.semaphore_wait(barrier, count + shots - 2)

    def slab_copy(source, target):
        return pltpu.make_async_remote_copy(
            src_ref=packet.at[target],
            dst_ref=gathered.at[shot, source],
            send_sem=slab_send.at[target],
            recv_sem=slab_recv.at[source],
            device_id=(shot, target),
            device_id_type=MESH,
        )

    def shot_copy(source, target):
        return pltpu.make_async_remote_copy(
            src_ref=gathered.at[source],
            dst_ref=gathered.at[source],
            send_sem=shot_send.at[target],
            recv_sem=shot_recv.at[source],
            device_id=(target, me),
            device_id_type=MESH,
        )

    def over_slabs(act):
        def run(offset, carry):
            act((me + offset) % count)
            return carry

        lax.fori_loop(1, count, run, 0)

    def over_shots(act):
        def run(offset, carry):
            act((shot + offset) % shots)
            return carry

        lax.fori_loop(1, shots, run, 0)

    def transfer(which, step, side, chunk):
        span = pl.ds(chunk * part, part)
        return pltpu.make_async_remote_copy(
            src_ref=edge.at[which, step, side, span],
            dst_ref=halo.at[which, step, 1 - side, span],
            send_sem=send_sem.at[which, step, side, chunk],
            recv_sem=recv_sem.at[which, step, 1 - side, chunk],
            device_id=(shot, me - 1 + 2 * side),
            device_id_type=MESH,
        )

    def send(which, step, chunk):
        @pl.when(me > 0)
        def _():
            transfer(which, step, 0, chunk).start()

        @pl.when(me < count - 1)
        def _():
            transfer(which, step, 1, chunk).start()

    def receive(which, step, chunk):
        @pl.when(me > 0)
        def _():
            transfer(which, step, 1, chunk).wait_recv()

        @pl.when(me < count - 1)
        def _():
            transfer(which, step, 0, chunk).wait_recv()

    def move(kind, p, source, target, device):
        return pltpu.make_async_remote_copy(
            src_ref=source,
            dst_ref=target,
            send_sem=move_send.at[kind, p],
            recv_sem=move_recv.at[kind, p],
            device_id=(device, me),
            device_id_type=MESH,
        )

    def model_across(p):
        span = model.at[pl.ds(shot * block + p * piece, piece)]
        return move(0, p, speed_in.at[pl.ds(p * piece, piece)], span, across)

    def model_partner(p):
        span = model.at[pl.ds(shot * block + p * piece, piece)]
        return move(1, p, speed_in.at[pl.ds(p * piece, piece)], span, partner)

    def model_onward(p):
        span = model.at[pl.ds(across * block + p * piece, piece)]
        return move(2, p, span, span, partner)

    for p in range(PIECES):
        model_across(p).start()
    over_slabs(lambda other: slab_copy(me, other).start())

    for which in range(2):
        loads[which].wait()
        for chunk in range(CHUNKS):
            def pack(i, carry):
                y = chunk * part + i * 8
                cell = field[which, 1, pl.ds(y + 2, 8)]
                edge[which, 0, 0, pl.ds(y, 8)] = cell[:, 0:2]
                edge[which, 0, 1, pl.ds(y, 8)] = cell[:, cells - 2 : cells]
                return carry

            lax.fori_loop(0, part // 8, pack, 0)
            send(which, 0, chunk)

    for p in range(PIECES):
        model_partner(p).start()
    for load in loads[2:]:
        load.wait()
    over_slabs(lambda other: slab_copy(other, other).wait_recv())
    over_shots(lambda other: shot_copy(shot, other).start())

    def build():
        over_shots(lambda other: shot_copy(other, other).wait_recv())
        listed = shots * count * gathered.shape[2]
        samples = gathered[...].reshape(listed, depth)
        row = lax.broadcasted_iota(jnp.int32, (1, listed), 1)
        mine = (row % gathered.shape[2]) // CAP == shot
        place = jnp.where(mine, samples.T[NSTEP : NSTEP + 1].astype(jnp.int32), -1)
        band = 16 * cells
        cell = lax.broadcasted_iota(jnp.int32, (band, listed), 0)

        def fill(i, carry):
            chosen = jnp.where(cell + i * band == place, 1.0, 0.0)
            plane = jnp.dot(
                chosen, samples,
                precision=lax.Precision.HIGHEST, preferred_element_type=jnp.float32,
            )
            drive[pl.ds(i * 16, 16)] = plane.reshape(16, cells, depth)
            return carry

        lax.fori_loop(0, rows // 16, fill, 0)

    for p in range(PIECES):
        model_across(p).wait_recv()
        model_onward(p).start()
        if p == 1:
            build()
    for p in range(PIECES):
        model_partner(p).wait_recv()
        model_onward(p).wait_recv()

    lane = lax.broadcasted_iota(jnp.int32, (ROWS, cells, depth), 2)

    def advance(which, k, image, last):
        newer, older, target = slot_of(k - 1), slot_of(k - 2), slot_of(k)
        partner = slot_of(k) if which == 0 else slot_of(NSTEP + 1 - k)
        for chunk in range(CHUNKS):
            receive(which, k - 1, chunk)

            def body(i, carry):
                y = chunk * part + i * ROWS
                window = field[which, newer, pl.ds(y, ROWS + 4)]
                core = window[2 : ROWS + 2]
                left = halo[which, k - 1, 0, pl.ds(y, ROWS)]
                right = halo[which, k - 1, 1, pl.ds(y, ROWS)]
                near = window[1 : ROWS + 1] + window[3 : ROWS + 3]
                far = window[0:ROWS] + window[4 : ROWS + 4]
                near = near + jnp.concatenate([left[:, 1:2], core[:, : cells - 1]], axis=1)
                near = near + jnp.concatenate([core[:, 1:], right[:, 0:1]], axis=1)
                far = far + jnp.concatenate([left, core[:, : cells - 2]], axis=1)
                far = far + jnp.concatenate([core[:, 2:], right], axis=1)
                near = near + jnp.where(lane >= 1, pltpu.roll(core, 1, 2), 0.0)
                near = near + jnp.where(lane < depth - 1, pltpu.roll(core, depth - 1, 2), 0.0)
                far = far + jnp.where(lane >= 2, pltpu.roll(core, 2, 2), 0.0)
                far = far + jnp.where(lane < depth - 2, pltpu.roll(core, depth - 2, 2), 0.0)
                lap = 3.0 * centre_coef * core + near_coef * near + far_coef * far
                if which == 1:
                    samples = drive[pl.ds(y, ROWS)]
                    shift = (RDEPTH - NSTEP + k + depth) % depth
                    lap = lap + jnp.where(lane == RDEPTH, pltpu.roll(samples, shift, 2), 0.0)
                older_cell = field[which, older, pl.ds(y + 2, ROWS)]
                value = 2.0 * core - older_cell + model[pl.ds(anchor + y, ROWS)] * lap
                if image:
                    if which == 0:
                        other = field[1, slot_of(NSTEP + 1 - k), pl.ds(y + 2, ROWS)]
                    else:
                        other = field[0, slot_of(NSTEP + 1 - k), pl.ds(y + 2, ROWS)]
                    if image == "first" and which == 0:
                        total[pl.ds(y + GROUP, ROWS)] = value * other
                    else:
                        total[pl.ds(y + GROUP, ROWS)] += value * other
                if not last:
                    field[which, target, pl.ds(y + 2, ROWS)] = value
                    edge[which, k, 0, pl.ds(y, ROWS)] = value[:, 0:2]
                    edge[which, k, 1, pl.ds(y, ROWS)] = value[:, cells - 2 : cells]
                return carry

            lax.fori_loop(0, part // ROWS, body, 0)
            if not last:
                send(which, k, chunk)

    def early(k, carry):
        advance(0, k, None, False)
        advance(1, k, None, False)
        return carry

    lax.fori_loop(1, HALF + 1, early, 0)
    advance(0, HALF + 1, "first", False)
    advance(1, HALF + 1, "first", False)

    def later(k, carry):
        advance(0, k, "more", False)
        advance(1, k, "more", False)
        return carry

    lax.fori_loop(HALF + 2, NSTEP, later, 0)
    advance(0, NSTEP, "more", True)
    advance(1, NSTEP, "more", True)

    over_slabs(lambda other: slab_copy(me, other).wait_send())
    over_shots(lambda other: shot_copy(shot, other).wait_send())
    for p in range(PIECES):
        model_across(p).wait_send()
        model_partner(p).wait_send()
        model_onward(p).wait_send()

    def share(owner, start):
        first = jnp.clip(owner * block + start - anchor, -GROUP, rows) + GROUP
        return total[pl.ds(first, GROUP)]

    def per_group(p, body):
        def run(i, carry):
            body(p * piece + i * GROUP)
            return carry

        lax.fori_loop(0, piece // GROUP, run, 0)

    def pair_copy(kind, p):
        return move(
            3 + kind, p,
            model.at[pl.ds(kind * block + p * piece, piece)],
            inbox.at[kind, pl.ds(p * piece, piece)],
            partner,
        )

    def far_copy(p):
        return move(
            5, p,
            model.at[pl.ds(2 * block + p * piece, piece)],
            arrived.at[pl.ds(p * piece, piece)],
            across,
        )

    for kind, owner in ((0, beyond), (1, partner)):
        for p in range(PIECES):
            def fill(y):
                model[pl.ds(kind * block + y, GROUP)] = share(owner, y)

            per_group(p, fill)
            pair_copy(kind, p).start()
        if kind == 0:
            for p in range(PIECES):
                pair_copy(0, p).wait_recv()

                def combine(y):
                    model[pl.ds(2 * block + y, GROUP)] = (
                        share(across, y) + inbox[0, pl.ds(y, GROUP)]
                    )

                per_group(p, combine)
                far_copy(p).start()
    for p in range(PIECES):
        pair_copy(1, p).wait_recv()

        def own(y):
            out_ref[pl.ds(y, GROUP)] = share(shot, y) + inbox[1, pl.ds(y, GROUP)]

        per_group(p, own)
    for p in range(PIECES):
        far_copy(p).wait_recv()

        def finish(y):
            out_ref[pl.ds(y, GROUP)] += arrived[pl.ds(y, GROUP)]

        per_group(p, finish)
    for p in range(PIECES):
        pair_copy(0, p).wait_send()
        pair_copy(1, p).wait_send()
        far_copy(p).wait_send()

    def settle(step, carry):
        for which in range(2):
            for chunk in range(CHUNKS):
                @pl.when(me > 0)
                def _():
                    transfer(which, step, 0, chunk).wait_send()

                @pl.when(me < count - 1)
                def _():
                    transfer(which, step, 1, chunk).wait_send()

        return carry

    lax.fori_loop(0, NSTEP, settle, 0)


def waves(anchors, prev, now, late, last, speed_model, packet):
    rows, cells, depth = now.shape
    block = speed_model.shape[0]
    model_rows = block * lax.axis_size("shot")
    anywhere = pl.BlockSpec(memory_space=pl.ANY)
    return pl.pallas_call(
        wave_kernel,
        out_shape=jax.ShapeDtypeStruct((block, cells, depth), jnp.float32),
        in_specs=[pl.BlockSpec(memory_space=pltpu.SMEM)] + [anywhere] * 6,
        out_specs=pl.BlockSpec(memory_space=pltpu.VMEM),
        scratch_shapes=[
            pltpu.VMEM((2, SLOTS, rows + 4, cells, depth), jnp.float32),
            pltpu.VMEM((2, NSTEP, 2, rows, 2, depth), jnp.float32),
            pltpu.VMEM((2, NSTEP, 2, rows, 2, depth), jnp.float32),
            pltpu.VMEM((model_rows, cells, depth), jnp.float32),
            pltpu.VMEM((rows, cells, depth), jnp.float32),
            pltpu.VMEM((rows + 2 * GROUP, cells, depth), jnp.float32),
            pltpu.VMEM((2, block, cells, depth), jnp.float32),
            pltpu.VMEM((block, cells, depth), jnp.float32),
            pltpu.VMEM((lax.axis_size("shot"),) + packet.shape, jnp.float32),
            pltpu.SemaphoreType.DMA((6,)),
            pltpu.SemaphoreType.DMA((2, NSTEP, 2, CHUNKS)),
            pltpu.SemaphoreType.DMA((2, NSTEP, 2, CHUNKS)),
            pltpu.SemaphoreType.DMA((6, PIECES)),
            pltpu.SemaphoreType.DMA((6, PIECES)),
            pltpu.SemaphoreType.DMA((lax.axis_size("slab"),)),
            pltpu.SemaphoreType.DMA((lax.axis_size("slab"),)),
            pltpu.SemaphoreType.DMA((lax.axis_size("shot"),)),
            pltpu.SemaphoreType.DMA((lax.axis_size("shot"),)),
        ],
        compiler_params=pltpu.CompilerParams(
            collective_id=0, has_side_effects=True, vmem_limit_bytes=61 * 1024 * 1024
        ),
        name="waves",
    )(anchors, prev, now, late, last, speed_model, packet)


def per_device(fwd_prev, fwd_now, adj_late, adj_last, speed_model, anchors, traces, dest, rec_pos):
    prev, now = (fwd_prev[0], fwd_now[0])
    late, last = (adj_late[0], adj_last[0])
    depth = now.shape[2]
    shots, slabs = lax.axis_size("shot"), lax.axis_size("slab")

    target = dest[:, 0]
    index = jnp.arange(target.shape[0], dtype=jnp.int32)
    ahead = (target[:, None] == target[None, :]) & (index[None, :] < index[:, None])
    rank = jnp.sum(ahead.astype(jnp.int32), axis=1)
    slot = ((target % slabs) * shots + target // slabs) * CAP + rank
    listing = jnp.concatenate([traces, rec_pos.astype(jnp.float32)[None, :]], axis=0)
    wide = jnp.pad(listing.T, ((0, 0), (0, depth - NSTEP - 1)))
    packet = jnp.zeros((slabs * shots * CAP, depth), jnp.float32).at[slot].set(wide)
    packet = packet.reshape(slabs, shots * CAP, depth)
    return waves(anchors, prev, now, late, last, speed_model, packet)


def solution(mesh):
    placed = (
        P("shot", None, "slab", None),
        P("shot", None, "slab", None),
        P("shot", None, "slab", None),
        P("shot", None, "slab", None),
        P("shot", "slab", None),
        P(),
        P(None, ("shot", "slab")),
        P(("shot", "slab"), None),
        P(("shot", "slab")),
    )
    return jax.shard_map(
        per_device, mesh=mesh, in_specs=placed, out_specs=P("shot", "slab", None), check_vma=False
    )
```

```python
import functools

import jax
import jax.numpy as jnp
from jax import lax
from jax.experimental import pallas as pl
from jax.experimental.pallas import tpu as pltpu
from jax.sharding import PartitionSpec as P

NSTEP = 8
HALF = NSTEP // 2
CAP = 2
RDEPTH = 3
ROWS = 4
CHUNKS = 2
SLOTS = HALF + 2
PIECES = 4
GROUP = 8

centre_coef = -2.5
near_coef = 4.0 / 3.0
far_coef = -1.0 / 12.0

MESH = pl.DeviceIdType.MESH


def slot_of(n):
    late = (n + 1) // SLOTS
    return (n + 1) * (1 - late) + ((n + 1) % 2) * late


def wave_kernel(
    anchors, fwd_prev, fwd_now, adj_late, adj_last, speed_in, packet,
    out_ref,
    field, halo, edge, model, drive, total, inbox, arrived, gathered,
    load_sem, send_sem, recv_sem, move_send, move_recv,
    slab_send, slab_recv, shot_send, shot_recv,
):
    count = lax.axis_size("slab")
    me = lax.axis_index("slab")
    shot = lax.axis_index("shot")
    rows, cells, depth = drive.shape
    block = out_ref.shape[0]
    piece = block // PIECES
    part = rows // CHUNKS
    core_index = shot % 2
    partner = shot + 1 - 2 * core_index
    across = (shot + 2) % 4
    beyond = (partner + 2) % 4
    anchor = anchors[shot]

    loads = [
        pltpu.make_async_copy(fwd_now, field.at[0, 1, pl.ds(2, rows)], load_sem.at[0]),
        pltpu.make_async_copy(adj_last, field.at[1, 1, pl.ds(2, rows)], load_sem.at[1]),
        pltpu.make_async_copy(fwd_prev, field.at[0, 0, pl.ds(2, rows)], load_sem.at[2]),
        pltpu.make_async_copy(speed_in, model.at[pl.ds(shot * block, block)], load_sem.at[3]),
        pltpu.make_async_copy(adj_late, field.at[1, 0, pl.ds(2, rows)], load_sem.at[4]),
        pltpu.make_async_copy(packet.at[me], gathered.at[shot, me], load_sem.at[5]),
    ]
    for load in loads:
        load.start()

    barrier = pltpu.get_barrier_semaphore()

    shots = gathered.shape[0]

    def greet_slab(offset, carry):
        other = (me + offset) % count
        pl.semaphore_signal(barrier, inc=1, device_id=(shot, other), device_id_type=MESH)
        return carry

    def greet_shot(offset, carry):
        other = (shot + offset) % shots
        pl.semaphore_signal(barrier, inc=1, device_id=(other, me), device_id_type=MESH)
        return carry

    lax.fori_loop(1, count, greet_slab, 0)
    lax.fori_loop(1, shots, greet_shot, 0)

    border = jnp.zeros((2, cells, depth), jnp.float32)
    total[0:GROUP] = jnp.zeros((GROUP, cells, depth), jnp.float32)
    total[rows + GROUP : rows + 2 * GROUP] = jnp.zeros((GROUP, cells, depth), jnp.float32)
    for which in range(2):
        for slot in range(SLOTS):
            field[which, slot, 0:2] = border
            field[which, slot, rows + 2 : rows + 4] = border

    def clear(side):
        def body(i, carry):
            for which in range(2):
                for step in range(NSTEP):
                    halo[which, step, side, pl.ds(i * 16, 16)] = jnp.zeros(
                        (16, 2, depth), jnp.float32
                    )
            return carry

        lax.fori_loop(0, rows // 16, body, 0)

    @pl.when(me == 0)
    def _():
        clear(0)

    @pl.when(me == count - 1)
    def _():
        clear(1)

    pl.semaphore_wait(barrier, count + shots - 2)

    def slab_copy(source, target):
        return pltpu.make_async_remote_copy(
            src_ref=packet.at[target],
            dst_ref=gathered.at[shot, source],
            send_sem=slab_send.at[target],
            recv_sem=slab_recv.at[source],
            device_id=(shot, target),
            device_id_type=MESH,
        )

    def shot_copy(source, target):
        return pltpu.make_async_remote_copy(
            src_ref=gathered.at[source],
            dst_ref=gathered.at[source],
            send_sem=shot_send.at[target],
            recv_sem=shot_recv.at[source],
            device_id=(target, me),
            device_id_type=MESH,
        )

    def over_slabs(act):
        def run(offset, carry):
            act((me + offset) % count)
            return carry

        lax.fori_loop(1, count, run, 0)

    def over_shots(act):
        def run(offset, carry):
            act((shot + offset) % shots)
            return carry

        lax.fori_loop(1, shots, run, 0)

    def transfer(which, step, side, chunk):
        span = pl.ds(chunk * part, part)
        return pltpu.make_async_remote_copy(
            src_ref=edge.at[which, step, side, span],
            dst_ref=halo.at[which, step, 1 - side, span],
            send_sem=send_sem.at[which, step, side, chunk],
            recv_sem=recv_sem.at[which, step, 1 - side, chunk],
            device_id=(shot, me - 1 + 2 * side),
            device_id_type=MESH,
        )

    def send(which, step, chunk):
        @pl.when(me > 0)
        def _():
            transfer(which, step, 0, chunk).start()

        @pl.when(me < count - 1)
        def _():
            transfer(which, step, 1, chunk).start()

    def receive(which, step, chunk):
        @pl.when(me > 0)
        def _():
            transfer(which, step, 1, chunk).wait_recv()

        @pl.when(me < count - 1)
        def _():
            transfer(which, step, 0, chunk).wait_recv()

    def move(kind, p, source, target, device):
        return pltpu.make_async_remote_copy(
            src_ref=source,
            dst_ref=target,
            send_sem=move_send.at[kind, p],
            recv_sem=move_recv.at[kind, p],
            device_id=(device, me),
            device_id_type=MESH,
        )

    def model_across(p):
        span = model.at[pl.ds(shot * block + p * piece, piece)]
        return move(0, p, speed_in.at[pl.ds(p * piece, piece)], span, across)

    def model_partner(p):
        span = model.at[pl.ds(shot * block + p * piece, piece)]
        return move(1, p, speed_in.at[pl.ds(p * piece, piece)], span, partner)

    def model_onward(p):
        span = model.at[pl.ds(across * block + p * piece, piece)]
        return move(2, p, span, span, partner)

    for p in range(PIECES):
        model_across(p).start()
    over_slabs(lambda other: slab_copy(me, other).start())

    for which in range(2):
        loads[which].wait()
        for chunk in range(CHUNKS):
            def pack(i, carry):
                y = chunk * part + i * 8
                cell = field[which, 1, pl.ds(y + 2, 8)]
                edge[which, 0, 0, pl.ds(y, 8)] = cell[:, 0:2]
                edge[which, 0, 1, pl.ds(y, 8)] = cell[:, cells - 2 : cells]
                return carry

            lax.fori_loop(0, part // 8, pack, 0)
            send(which, 0, chunk)

    for p in range(PIECES):
        model_partner(p).start()
    for load in loads[2:]:
        load.wait()
    over_slabs(lambda other: slab_copy(other, other).wait_recv())
    over_shots(lambda other: shot_copy(shot, other).start())

    def build():
        over_shots(lambda other: shot_copy(other, other).wait_recv())
        listed = shots * count * gathered.shape[2]
        samples = gathered[...].reshape(listed, depth)
        row = lax.broadcasted_iota(jnp.int32, (1, listed), 1)
        mine = (row % gathered.shape[2]) // CAP == shot
        place = jnp.where(mine, samples.T[NSTEP : NSTEP + 1].astype(jnp.int32), -1)
        band = 16 * cells
        cell = lax.broadcasted_iota(jnp.int32, (band, listed), 0)

        def fill(i, carry):
            chosen = jnp.where(cell + i * band == place, 1.0, 0.0)
            plane = jnp.dot(
                chosen, samples,
                precision=lax.Precision.HIGHEST, preferred_element_type=jnp.float32,
            )
            drive[pl.ds(i * 16, 16)] = plane.reshape(16, cells, depth)
            return carry

        lax.fori_loop(0, rows // 16, fill, 0)

    for p in range(PIECES):
        model_across(p).wait_recv()
        model_onward(p).start()
    for p in range(PIECES):
        model_partner(p).wait_recv()
        model_onward(p).wait_recv()

    lane = lax.broadcasted_iota(jnp.int32, (ROWS, cells, depth), 2)

    def advance(which, k, image, last):
        newer, older, target = slot_of(k - 1), slot_of(k - 2), slot_of(k)
        partner = slot_of(k) if which == 0 else slot_of(NSTEP + 1 - k)
        for chunk in range(CHUNKS):
            receive(which, k - 1, chunk)

            def body(i, carry):
                y = chunk * part + i * ROWS
                window = field[which, newer, pl.ds(y, ROWS + 4)]
                core = window[2 : ROWS + 2]
                left = halo[which, k - 1, 0, pl.ds(y, ROWS)]
                right = halo[which, k - 1, 1, pl.ds(y, ROWS)]
                near = window[1 : ROWS + 1] + window[3 : ROWS + 3]
                far = window[0:ROWS] + window[4 : ROWS + 4]
                near = near + jnp.concatenate([left[:, 1:2], core[:, : cells - 1]], axis=1)
                near = near + jnp.concatenate([core[:, 1:], right[:, 0:1]], axis=1)
                far = far + jnp.concatenate([left, core[:, : cells - 2]], axis=1)
                far = far + jnp.concatenate([core[:, 2:], right], axis=1)
                near = near + jnp.where(lane >= 1, pltpu.roll(core, 1, 2), 0.0)
                near = near + jnp.where(lane < depth - 1, pltpu.roll(core, depth - 1, 2), 0.0)
                far = far + jnp.where(lane >= 2, pltpu.roll(core, 2, 2), 0.0)
                far = far + jnp.where(lane < depth - 2, pltpu.roll(core, depth - 2, 2), 0.0)
                lap = 3.0 * centre_coef * core + near_coef * near + far_coef * far
                if which == 1:
                    samples = drive[pl.ds(y, ROWS)]
                    shift = (RDEPTH - NSTEP + k + depth) % depth
                    lap = lap + jnp.where(lane == RDEPTH, pltpu.roll(samples, shift, 2), 0.0)
                older_cell = field[which, older, pl.ds(y + 2, ROWS)]
                value = 2.0 * core - older_cell + model[pl.ds(anchor + y, ROWS)] * lap
                if image:
                    if which == 0:
                        other = field[1, slot_of(NSTEP + 1 - k), pl.ds(y + 2, ROWS)]
                    else:
                        other = field[0, slot_of(NSTEP + 1 - k), pl.ds(y + 2, ROWS)]
                    if image == "first" and which == 0:
                        total[pl.ds(y + GROUP, ROWS)] = value * other
                    else:
                        total[pl.ds(y + GROUP, ROWS)] += value * other
                if not last:
                    field[which, target, pl.ds(y + 2, ROWS)] = value
                    edge[which, k, 0, pl.ds(y, ROWS)] = value[:, 0:2]
                    edge[which, k, 1, pl.ds(y, ROWS)] = value[:, cells - 2 : cells]
                return carry

            lax.fori_loop(0, part // ROWS, body, 0)
            if not last:
                send(which, k, chunk)

    def early(k, carry):
        advance(0, k, None, False)
        advance(1, k, None, False)
        return carry

    advance(0, 1, None, False)
    build()
    advance(1, 1, None, False)
    lax.fori_loop(2, HALF + 1, early, 0)
    advance(0, HALF + 1, "first", False)
    advance(1, HALF + 1, "first", False)

    def later(k, carry):
        advance(0, k, "more", False)
        advance(1, k, "more", False)
        return carry

    lax.fori_loop(HALF + 2, NSTEP, later, 0)
    advance(0, NSTEP, "more", True)
    advance(1, NSTEP, "more", True)

    over_slabs(lambda other: slab_copy(me, other).wait_send())
    over_shots(lambda other: shot_copy(shot, other).wait_send())
    for p in range(PIECES):
        model_across(p).wait_send()
        model_partner(p).wait_send()
        model_onward(p).wait_send()

    def share(owner, start):
        first = jnp.clip(owner * block + start - anchor, -GROUP, rows) + GROUP
        return total[pl.ds(first, GROUP)]

    def per_group(p, body):
        def run(i, carry):
            body(p * piece + i * GROUP)
            return carry

        lax.fori_loop(0, piece // GROUP, run, 0)

    def pair_copy(kind, p):
        return move(
            3 + kind, p,
            model.at[pl.ds(kind * block + p * piece, piece)],
            inbox.at[kind, pl.ds(p * piece, piece)],
            partner,
        )

    def far_copy(p):
        return move(
            5, p,
            model.at[pl.ds(2 * block + p * piece, piece)],
            arrived.at[pl.ds(p * piece, piece)],
            across,
        )

    for kind, owner in ((0, beyond), (1, partner)):
        for p in range(PIECES):
            def fill(y):
                model[pl.ds(kind * block + y, GROUP)] = share(owner, y)

            per_group(p, fill)
            pair_copy(kind, p).start()
        if kind == 0:
            for p in range(PIECES):
                pair_copy(0, p).wait_recv()

                def combine(y):
                    model[pl.ds(2 * block + y, GROUP)] = (
                        share(across, y) + inbox[0, pl.ds(y, GROUP)]
                    )

                per_group(p, combine)
                far_copy(p).start()
    for p in range(PIECES):
        pair_copy(1, p).wait_recv()

        def own(y):
            out_ref[pl.ds(y, GROUP)] = share(shot, y) + inbox[1, pl.ds(y, GROUP)]

        per_group(p, own)
    for p in range(PIECES):
        far_copy(p).wait_recv()

        def finish(y):
            out_ref[pl.ds(y, GROUP)] += arrived[pl.ds(y, GROUP)]

        per_group(p, finish)
    for p in range(PIECES):
        pair_copy(0, p).wait_send()
        pair_copy(1, p).wait_send()
        far_copy(p).wait_send()

    def settle(step, carry):
        for which in range(2):
            for chunk in range(CHUNKS):
                @pl.when(me > 0)
                def _():
                    transfer(which, step, 0, chunk).wait_send()

                @pl.when(me < count - 1)
                def _():
                    transfer(which, step, 1, chunk).wait_send()

        return carry

    lax.fori_loop(0, NSTEP, settle, 0)


def waves(anchors, prev, now, late, last, speed_model, packet):
    rows, cells, depth = now.shape
    block = speed_model.shape[0]
    model_rows = block * lax.axis_size("shot")
    anywhere = pl.BlockSpec(memory_space=pl.ANY)
    return pl.pallas_call(
        wave_kernel,
        out_shape=jax.ShapeDtypeStruct((block, cells, depth), jnp.float32),
        in_specs=[pl.BlockSpec(memory_space=pltpu.SMEM)] + [anywhere] * 6,
        out_specs=pl.BlockSpec(memory_space=pltpu.VMEM),
        scratch_shapes=[
            pltpu.VMEM((2, SLOTS, rows + 4, cells, depth), jnp.float32),
            pltpu.VMEM((2, NSTEP, 2, rows, 2, depth), jnp.float32),
            pltpu.VMEM((2, NSTEP, 2, rows, 2, depth), jnp.float32),
            pltpu.VMEM((model_rows, cells, depth), jnp.float32),
            pltpu.VMEM((rows, cells, depth), jnp.float32),
            pltpu.VMEM((rows + 2 * GROUP, cells, depth), jnp.float32),
            pltpu.VMEM((2, block, cells, depth), jnp.float32),
            pltpu.VMEM((block, cells, depth), jnp.float32),
            pltpu.VMEM((lax.axis_size("shot"),) + packet.shape, jnp.float32),
            pltpu.SemaphoreType.DMA((6,)),
            pltpu.SemaphoreType.DMA((2, NSTEP, 2, CHUNKS)),
            pltpu.SemaphoreType.DMA((2, NSTEP, 2, CHUNKS)),
            pltpu.SemaphoreType.DMA((6, PIECES)),
            pltpu.SemaphoreType.DMA((6, PIECES)),
            pltpu.SemaphoreType.DMA((lax.axis_size("slab"),)),
            pltpu.SemaphoreType.DMA((lax.axis_size("slab"),)),
            pltpu.SemaphoreType.DMA((lax.axis_size("shot"),)),
            pltpu.SemaphoreType.DMA((lax.axis_size("shot"),)),
        ],
        compiler_params=pltpu.CompilerParams(
            collective_id=0, has_side_effects=True, vmem_limit_bytes=61 * 1024 * 1024
        ),
        name="waves",
    )(anchors, prev, now, late, last, speed_model, packet)


def per_device(fwd_prev, fwd_now, adj_late, adj_last, speed_model, anchors, traces, dest, rec_pos):
    prev, now = (fwd_prev[0], fwd_now[0])
    late, last = (adj_late[0], adj_last[0])
    depth = now.shape[2]
    shots, slabs = lax.axis_size("shot"), lax.axis_size("slab")

    target = dest[:, 0]
    index = jnp.arange(target.shape[0], dtype=jnp.int32)
    ahead = (target[:, None] == target[None, :]) & (index[None, :] < index[:, None])
    rank = jnp.sum(ahead.astype(jnp.int32), axis=1)
    slot = ((target % slabs) * shots + target // slabs) * CAP + rank
    listing = jnp.concatenate([traces, rec_pos.astype(jnp.float32)[None, :]], axis=0)
    wide = jnp.pad(listing.T, ((0, 0), (0, depth - NSTEP - 1)))
    packet = jnp.zeros((slabs * shots * CAP, depth), jnp.float32).at[slot].set(wide)
    packet = packet.reshape(slabs, shots * CAP, depth)
    return waves(anchors, prev, now, late, last, speed_model, packet)


def solution(mesh):
    placed = (
        P("shot", None, "slab", None),
        P("shot", None, "slab", None),
        P("shot", None, "slab", None),
        P("shot", None, "slab", None),
        P("shot", "slab", None),
        P(),
        P(None, ("shot", "slab")),
        P(("shot", "slab"), None),
        P(("shot", "slab")),
    )
    return jax.shard_map(
        per_device, mesh=mesh, in_specs=placed, out_specs=P("shot", "slab", None), check_vma=False
    )
```
